128 devices in a mesh: trow: 4 (over x_lo, core), tcol: 4 (over z), visit: 8 (over x_hi, y).
Axes of the slice: x: 4 (x_hi: 2, x_lo: 2; x = x_hi * 2 + x_lo), y: 4, z: 4, core: 2. Of those that a mesh axis runs over, the one named last changes fastest.
Arguments:
- template: float32 [2048, 2048], P(('trow', 'visit'), 'tcol'), may hold values from -6 to 6
- warped: float32 [1536, 256, 256], P(('trow', 'tcol', 'visit')), may hold values from -6 to 6
- coeffs: float32 [1536, 27, 3], P(('trow', 'tcol', 'visit')), may hold values from -2 to 2
- dest_tile: int32 [1536, 1], P(('trow', 'tcol', 'visit')), may hold values from 0 to 15; in each aligned block of 12 rows (0 to 11, 12 to 23, ...) at most 2 rows name the same one
- position: int32 [1536, 1], P(('trow', 'tcol', 'visit')), may hold values from 0 to 3
Outputs:
- difference: float32 [1536, 256, 256], P(('trow', 'tcol', 'visit'))
The draws below stay inside these ranges and needn't reach their ends.
Inputs may be any that keep to these rules, and one draw needn't show every extreme that they name: `dest_tile`: tile index = tract row times the number of tract columns plus tract column; among the 12 blocks of one device no tile is named more than 2 times. `position`: sub-block row times 512 / 256 plus sub-block column.
All inputs are finite; a program needn't handle non-finite values.
Results may differ from the reference program's by a relative error of at most 0.0003.
Values sent between devices are 32-bit elements; how exact they have to be, the bound alone decides.
No kernel may reach another device: no remote copies, remote signals or barrier semaphores. Data moves between devices by JAX's collectives and lax.ppermute only.
A program may use at most 192 MiB of HBM per device.

```python
import math
import jax
import jax.numpy as jnp
import numpy as np
from jax import lax

TILE = 512
BLK = 256
HALF = 10
NB = 12
CAP = 2
NR = 2048
NC = 2048
BLOCKS = 1536
N_TROW = 4
N_TCOL = 4


def set_ends(values, stream_key, low, largest):
    extent = values.shape
    index_at = [jax.random.randint(jax.random.fold_in(stream_key, axis), (), 0, extent[axis]) for axis in range(len(extent))]
    values = values.at[tuple(index_at)].set(low)
    longest = extent.index(max(extent))
    index_at[longest] = (index_at[longest] + 1) % extent[longest]
    return values.at[tuple(index_at)].set(largest)


def block_levels(key, dims, cuts, smallest, largest):
    def one(axis_at, shards_of):
        steps = jax.random.uniform(jax.random.fold_in(jax.random.fold_in(key, 6), axis_at), (shards_of,), jnp.float32, smallest / len(cuts), largest / len(cuts))
        return jnp.repeat(jnp.exp(steps), dims[axis_at] // shards_of).reshape((-1,) + (1,) * (len(dims) - axis_at - 1))

    factor_of = one(*cuts[0])
    for cut in cuts[1:]:
        factor_of = factor_of * one(*cut)
    return factor_of


def assign_block(key, own, number, rows, number_of, top, limit, slope):
    sequence = jax.random.permutation(key, number_of)
    crowded, common = load_shares(number_of, rows * top, limit, slope, True), load_shares(number_of, rows * top, limit, slope, False)
    places = jnp.arange(number_of)

    def named(lengths, offset_by):
        used = int((lengths > 0).sum())
        fixed = max(1, used // 4)
        moved = fixed + (places - fixed + offset_by * (used - fixed)) % max(1, number_of - fixed)
        return jnp.zeros((number_of,), jnp.int32).at[sequence[jnp.where(places < fixed, places, moved)]].set(jnp.asarray(lengths, jnp.int32))

    lengths = jnp.where(number % 4 == 0, named(crowded, number // 4), named(common, number - number // 4 - 1))
    mixed = jax.random.permutation(jax.random.fold_in(own, 3), number_of)
    source_of, receiver = mixed[0:number_of // 2 * 2:2], mixed[1:number_of // 2 * 2:2]
    slack = jnp.minimum(lengths[source_of] - 1, limit - lengths[receiver]) // 2
    slack = jnp.where((source_of == sequence[0]) | (receiver == sequence[0]) | (lengths[receiver] == 0), 0, jnp.maximum(slack, 0))
    moved = jax.random.randint(jax.random.fold_in(own, 4), (number_of // 2,), 0, 1 << 20) % (slack + 1)
    lengths = lengths.at[source_of].add(-moved).at[receiver].add(moved)
    items = jnp.searchsorted(jnp.cumsum(lengths), jnp.arange(rows * top), side="right").astype(jnp.int32)
    listing = items.reshape(top, rows).T
    listing = listing[jax.random.permutation(jax.random.fold_in(own, 1), rows)]
    offset_by = jax.random.randint(jax.random.fold_in(own, 2), (rows, 1), 0, top)
    return jnp.take_along_axis(listing, (jnp.arange(top)[None, :] + offset_by) % top, axis=1)


def load_shares(number_of, total, bound, lean, full):
    weights = [(1 << 20) // math.isqrt(standing ** lean) + 1 for standing in range(1, number_of + 1)]
    largest = bound if full else min(bound, max(-(-total // number_of), total * weights[0] // sum(weights)))
    least = 1 if total - largest >= number_of - 1 else 0
    counts, surplus = [largest] + [least] * (number_of - 1), total - largest - least * (number_of - 1)
    while surplus > 0:
        free = [i for i in range(1, number_of) if counts[i] < largest] or [i for i in range(1, number_of) if counts[i] < bound]
        pool, remaining = sum([weights[i] for i in free]), surplus
        for i in free:
            addition = min(bound - counts[i], max(1, remaining * weights[i] // pool), surplus)
            counts[i] = counts[i] + addition
            surplus = surplus - addition
    return np.array(counts)


def bell_draw(key, shape, deviation, reach, cuts=(), kind=jnp.bfloat16):
    level = block_levels(key, shape, cuts, -0.22, 0.18) if cuts else 1.0
    entries = jax.random.normal(key, shape, jnp.float32) * deviation * level
    return jnp.minimum(jnp.maximum(entries, -reach), reach).astype(kind)


def setup_inputs(seed: int = 0) -> dict:
    key_of = jax.random.split(jax.random.key(seed), 6)
    template = bell_draw(key_of[0], (NR, NC), 1.0, 6.0, ((0, 32), (1, 4)), jnp.float32)
    warped = bell_draw(key_of[1], (BLOCKS, BLK, BLK), 1.0, 6.0, ((0, 128),), jnp.float32)
    coeffs = bell_draw(key_of[2], (BLOCKS, 27, 3), 0.25, 2.0, ((0, 128),), jnp.float32)
    dest_tile_keys = jax.random.split(jax.random.fold_in(key_of[3], 1), BLOCKS // NB)
    dest_tile_turns = jax.random.permutation(jax.random.fold_in(key_of[3], 3), BLOCKS // NB)
    dest_tile = jax.vmap(lambda own, number: assign_block(jax.random.fold_in(key_of[3], 2), own, number, NB, N_TROW * N_TCOL, 1, CAP, 2))(dest_tile_keys, dest_tile_turns).reshape((BLOCKS, 1))
    position = set_ends(jax.random.randint(key_of[4], (BLOCKS, 1), 0, (TILE // BLK) * (TILE // BLK)), jax.random.fold_in(key_of[4], 1), 0, ((TILE // BLK) * (TILE // BLK)) - 1).astype(jnp.int32)
    return dict(template=template, warped=warped, coeffs=coeffs, dest_tile=dest_tile, position=position)


SPREADS = (1.0, 2.0, 4.0)
DEGREES = (4, 2, 2)

def taps_for(spread, power):
    offsets = jnp.arange(-HALF, HALF + 1).astype(jnp.float32)
    weights = jnp.exp(-offsets * offsets / (2.0 * spread * spread))
    for step in range(power):
        weights = weights * offsets
    return weights / jnp.sqrt(jnp.sum(weights * weights))

def band_matrix(tap_weights, length):
    row_ids = jnp.arange(length)[:, None]
    col_ids = jnp.arange(length + 2 * HALF)[None, :]
    offset = col_ids - row_ids
    matrix = jnp.zeros((length, length + 2 * HALF), jnp.float32)
    for tap_index in range(2 * HALF + 1):
        matrix = matrix + jnp.where(offset == tap_index, tap_weights[tap_index], 0.0)
    return matrix

def basis_images(window, out_rows, out_cols):
    highest = lax.Precision.HIGHEST
    stacked = []
    for spread, degree in zip(SPREADS, DEGREES):
        row_passes = [jnp.dot(band_matrix(taps_for(spread, power), out_rows), window, precision=highest) for power in range(degree + 1)]
        col_bands = [band_matrix(taps_for(spread, power), out_cols) for power in range(degree + 1)]
        for row_power in range(degree + 1):
            for col_power in range(degree + 1 - row_power):
                stacked.append(jnp.dot(row_passes[row_power], col_bands[col_power].T, precision=highest))
    return jnp.stack(stacked)

def block_model(images, coef_block, row_start, col_start):
    zero = jnp.int32(0)
    piece = lax.dynamic_slice(images, (zero, row_start.astype(jnp.int32), col_start.astype(jnp.int32)), (images.shape[0], BLK, BLK))
    mixed = jnp.einsum('bj,bxy->jxy', coef_block, piece, precision=lax.Precision.HIGHEST)
    coords = (jnp.arange(BLK).astype(jnp.float32) - (BLK - 1) / 2.0) / ((BLK - 1) / 2.0)
    return mixed[0] + coords[None, :] * mixed[1] + coords[:, None] * mixed[2]

def reference(template, warped, coeffs, dest_tile, position):
    padded = jnp.pad(template, HALF)
    subs = TILE // BLK

    def tile_images(tile_index):
        row_tile = tile_index // N_TCOL
        col_tile = tile_index % N_TCOL
        window = lax.dynamic_slice(padded, ((row_tile * TILE).astype(jnp.int32), (col_tile * TILE).astype(jnp.int32)), (TILE + 2 * HALF, TILE + 2 * HALF))
        return basis_images(window, TILE, TILE)
    images_all = lax.map(tile_images, jnp.arange(N_TROW * N_TCOL, dtype=jnp.int32))

    def block_difference(packed):
        image_block, coef_block, tile_id, sub_place = packed
        images = lax.dynamic_index_in_dim(images_all, tile_id.astype(jnp.int32), 0, keepdims=False)
        model = block_model(images, coef_block, sub_place // subs * BLK, sub_place % subs * BLK)
        return image_block - model
    return lax.map(block_difference, (warped, coeffs, dest_tile[:, 0], position[:, 0]))
```

```python
import functools

import jax
import jax.numpy as jnp
import numpy as np
from jax import lax
from jax.experimental import pallas as pl
from jax.experimental.pallas import tpu as pltpu
from jax.sharding import PartitionSpec as P

BLK = 256
TILE = 512
HALF = 10
SPREADS = (1.0, 2.0, 4.0)
DEGREES = (4, 2, 2)
FILTERS = [(s, k) for s, d in enumerate(DEGREES) for k in range(d + 1)]
NF = len(FILTERS)
BASIS = {}
for _s, _d in enumerate(DEGREES):
    for _i in range(_d + 1):
        for _j in range(_d + 1 - _i):
            BASIS[(_s, _i, _j)] = len(BASIS)
MAXI = max(DEGREES) + 1

M = 32
CH = 64
NT = BLK // M
KK = NF * CH
WR = 288
WC = 512
ROFF = 16 - HALF
COFF = 128 - HALF


def taps_for(spread, power):
    offsets = np.arange(-HALF, HALF + 1).astype(np.float32)
    weights = np.exp(-offsets * offsets / np.float32(2.0 * spread * spread)).astype(np.float32)
    for _ in range(power):
        weights = weights * offsets
    return (weights / np.sqrt(np.sum(weights * weights))).astype(np.float32)


def column_filters():
    out = np.zeros((256, NF, 128), np.float32)
    for f, (s, k) in enumerate(FILTERS):
        taps = taps_for(SPREADS[s], k)
        for y in range(128):
            out[y : y + 21, f, y] = taps
    return out.reshape(256, NF * 128)


def row_filters():
    out = np.zeros((MAXI, M, NF, CH), np.float32)
    for f, (s, k) in enumerate(FILTERS):
        for i in range(DEGREES[s] + 1 - k):
            taps = taps_for(SPREADS[s], i)
            for x in range(M):
                out[i, x, f, x + ROFF : x + ROFF + 21] = taps
    return out.reshape(MAXI, M, KK)


def split(value):
    high = value.astype(jnp.bfloat16)
    low = (value - high.astype(jnp.float32)).astype(jnp.bfloat16)
    return high, low


def mix_kernel(coef_ref, rows_ref, out_ref):
    def mixed(g):
        total = coef_ref[0, g, 0:1, :] * rows_ref[0]
        for i in range(1, MAXI):
            total = total + coef_ref[0, g, i : i + 1, :] * rows_ref[i]
        return total

    const, across, down = mixed(0), mixed(1), mixed(2)
    across_h, across_l = split(across)
    half = (BLK - 1) / 2.0
    for t in range(NT):
        row = lax.broadcasted_iota(jnp.int32, (M, 1), 0) + t * M
        weight = (row.astype(jnp.float32) - half) * (1.0 / half)
        high, low = split(const + weight * down)
        out_ref[0, t, 0:M, :] = high
        out_ref[0, t, M : 2 * M, :] = across_h
        out_ref[0, t, 2 * M : 3 * M, :] = low
        out_ref[0, t, 3 * M : 4 * M, :] = across_l


def mix_rows(coeffs):
    nb = coeffs.shape[0]
    index = np.zeros((MAXI, NF), np.int32)
    valid = np.zeros((MAXI, NF), np.float32)
    for f, (s, k) in enumerate(FILTERS):
        for i in range(DEGREES[s] + 1 - k):
            index[i, f] = BASIS[(s, i, k)]
            valid[i, f] = 1.0
    picked = jnp.stack(
        [jnp.stack([coeffs[:, int(index[i, f]), :] * float(valid[i, f]) for f in range(NF)], 1) for i in range(MAXI)], 1
    )
    lanes = jnp.repeat(jnp.transpose(picked, (0, 3, 1, 2)), CH, axis=3)
    return pl.pallas_call(
        mix_kernel,
        grid=(nb,),
        in_specs=[
            pl.BlockSpec((1, 3, MAXI, KK), lambda b: (b, 0, 0, 0)),
            pl.BlockSpec((MAXI, M, KK), lambda b: (0, 0, 0)),
        ],
        out_specs=pl.BlockSpec((1, NT, 4 * M, KK), lambda b: (b, 0, 0, 0)),
        out_shape=jax.ShapeDtypeStruct((nb, NT, 4 * M, KK), jnp.bfloat16),
        name="mix_rows",
        cost_estimate=pl.CostEstimate(flops=10**8, bytes_accessed=2 * 10**7, transcendentals=0),
    )(lanes, jnp.asarray(row_filters()))


def window_copies(n, tile_ref, pos_ref, image, window, sem, slot):
    tile, pos = tile_ref[n], pos_ref[n]
    r, c = tile // 4, tile % 4
    pr, pc = pos // 2, pos % 2
    rn = jnp.clip(r + 2 * pr - 1, 0, 3)
    cn = jnp.clip(c + 2 * pc - 1, 0, 3)
    rows = ((r, pl.multiple_of(pr * 240, 8), pl.multiple_of((1 - pr) * 16, 8), 272),
            (rn, pl.multiple_of((1 - pr) * 496, 8), pl.multiple_of(pr * 272, 8), 16))
    cols = ((c, pl.multiple_of(pc * 128, 128), pl.multiple_of((1 - pc) * 128, 128), 384),
            (cn, pl.multiple_of((1 - pc) * 384, 128), pl.multiple_of(pc * 384, 128), 128))
    out = []
    for a, (tr, src_r, dst_r, nr) in enumerate(rows):
        for b, (tc, src_c, dst_c, nc) in enumerate(cols):
            out.append(
                pltpu.make_async_copy(
                    image.at[tr * 4 + tc, pl.ds(src_r, nr), pl.ds(src_c, nc)],
                    window.at[slot, pl.ds(dst_r, nr), pl.ds(dst_c, nc)],
                    sem.at[slot, 2 * a + b],
                )
            )
    return out


def model_kernel(tile_ref, pos_ref, image, warped_ref, rows_ref, cols_ref, out_ref, window, vh, vl, sem):
    n = pl.program_id(0)
    count = pl.num_programs(0)
    slot = n % 2

    @pl.when(n == 0)
    def _():
        for copy in window_copies(n, tile_ref, pos_ref, image, window, sem, slot):
            copy.start()

    @pl.when(n + 1 < count)
    def _():
        for copy in window_copies(n + 1, tile_ref, pos_ref, image, window, sem, 1 - slot):
            copy.start()

    for copy in window_copies(n, tile_ref, pos_ref, image, window, sem, slot):
        copy.wait()

    tile, pos = tile_ref[n], pos_ref[n]
    r, c = tile // 4, tile % 4
    pr, pc = pos // 2, pos % 2

    @pl.when((r == 0) & (pr == 0))
    def _():
        window[slot, 0:16, :] = jnp.zeros((16, WC), jnp.float32)

    @pl.when((r == 3) & (pr == 1))
    def _():
        window[slot, 272:288, :] = jnp.zeros((16, WC), jnp.float32)

    @pl.when((c == 0) & (pc == 0))
    def _():
        window[slot, :, 0:128] = jnp.zeros((WR, 128), jnp.float32)

    @pl.when((c == 3) & (pc == 1))
    def _():
        window[slot, :, 384:512] = jnp.zeros((WR, 128), jnp.float32)

    rolled = pltpu.roll(window[slot], WC - COFF, axis=1)[:, 0:384]
    th, tl = split(rolled)
    for half in range(2):
        lhs = jnp.concatenate(
            [th[:, 128 * half : 128 * half + 256], tl[:, 128 * half : 128 * half + 256], th[:, 128 * half : 128 * half + 256]],
            axis=1,
        )
        for f in range(0, NF, 2):
            width = min(2, NF - f)
            value = jnp.dot(lhs, cols_ref[:, 128 * f : 128 * (f + width)], preferred_element_type=jnp.float32)
            for w in range(width):
                high, low = split(value[:, 128 * w : 128 * (w + 1)])
                vh[f + w, :, 128 * half : 128 * (half + 1)] = high
                vl[f + w, :, 128 * half : 128 * (half + 1)] = low

    mid = (BLK - 1) / 2.0
    across = (lax.broadcasted_iota(jnp.int32, (1, BLK), 1).astype(jnp.float32) - mid) * (1.0 / mid)

    def step(t, carry):
        start = pl.multiple_of(t * M, M)
        wh = vh[:, pl.ds(start, CH), :].reshape(KK, BLK)
        wl = vl[:, pl.ds(start, CH), :].reshape(KK, BLK)
        first = jnp.dot(rows_ref[0, t], wh, preferred_element_type=jnp.float32)
        second = jnp.dot(rows_ref[0, t, 0 : 2 * M, :], wl, preferred_element_type=jnp.float32)
        flat = first[0:M] + first[2 * M : 3 * M] + second[0:M]
        slope = first[M : 2 * M] + first[3 * M : 4 * M] + second[M : 2 * M]
        out_ref[0, pl.ds(start, M), :] = warped_ref[0, pl.ds(start, M), :] - (flat + across * slope)
        return carry

    lax.fori_loop(0, NT, step, 0)


def difference(images, warped, rows, tile, pos):
    nb = warped.shape[0]
    cols = jnp.asarray(column_filters())
    ch, cl = split(cols)
    consts = jnp.concatenate([ch, ch, cl], axis=0)
    spec = pltpu.PrefetchScalarGridSpec(
        num_scalar_prefetch=2,
        grid=(nb,),
        in_specs=[
            pl.BlockSpec(memory_space=pl.ANY),
            pl.BlockSpec((1, BLK, BLK), lambda b, *_: (b, 0, 0)),
            pl.BlockSpec((1, NT, 4 * M, KK), lambda b, *_: (b, 0, 0, 0)),
            pl.BlockSpec((768, NF * 128), lambda b, *_: (0, 0)),
        ],
        out_specs=pl.BlockSpec((1, BLK, BLK), lambda b, *_: (b, 0, 0)),
        scratch_shapes=[
            pltpu.VMEM((2, WR, WC), jnp.float32),
            pltpu.VMEM((NF, WR, BLK), jnp.bfloat16),
            pltpu.VMEM((NF, WR, BLK), jnp.bfloat16),
            pltpu.SemaphoreType.DMA((2, 4)),
        ],
    )
    return pl.pallas_call(
        model_kernel,
        grid_spec=spec,
        out_shape=jax.ShapeDtypeStruct((nb, BLK, BLK), jnp.float32),
        name="difference",
    )(tile, pos, images, warped, rows, consts)


def on_device(template, warped, coeffs, dest_tile, position):
    tile = lax.all_gather(template, "visit", axis=0, tiled=True)
    images = lax.all_gather(tile, ("trow", "tcol"), axis=0)
    rows = mix_rows(coeffs)
    return difference(images, warped, rows, dest_tile[:, 0], position[:, 0])


def solution(mesh):
    return jax.shard_map(
        on_device,
        mesh=mesh,
        in_specs=(
            P(("trow", "visit"), "tcol"),
            P(("trow", "tcol", "visit"), None, None),
            P(("trow", "tcol", "visit"), None, None),
            P(("trow", "tcol", "visit"), None),
            P(("trow", "tcol", "visit"), None),
        ),
        out_specs=P(("trow", "tcol", "visit"), None, None),
        check_vma=False,
    )
```

```python
import functools

import jax
import jax.numpy as jnp
import numpy as np
from jax import lax
from jax.experimental import pallas as pl
from jax.experimental.pallas import tpu as pltpu
from jax.sharding import PartitionSpec as P

BLK = 256
TILE = 512
HALF = 10
SPREADS = (1.0, 2.0, 4.0)
DEGREES = (4, 2, 2)
FILTERS = [(s, k) for s, d in enumerate(DEGREES) for k in range(d + 1)]
NF = len(FILTERS)
BASIS = {}
for _s, _d in enumerate(DEGREES):
    for _i in range(_d + 1):
        for _j in range(_d + 1 - _i):
            BASIS[(_s, _i, _j)] = len(BASIS)
MAXI = max(DEGREES) + 1

M = 32
CH = M + 32
SPAN = 84
LANES = 768
NT = BLK // M
KK = NF * CH
WR = 288
WC = 512
ROFF = 16 - HALF
COFF = 128 - HALF


def taps_for(spread, power):
    offsets = np.arange(-HALF, HALF + 1).astype(np.float32)
    weights = np.exp(-offsets * offsets / np.float32(2.0 * spread * spread)).astype(np.float32)
    for _ in range(power):
        weights = weights * offsets
    return (weights / np.sqrt(np.sum(weights * weights))).astype(np.float32)


def column_filters():
    one = np.zeros((SPAN, 12, 64), np.float32)
    for f, (s, k) in enumerate(FILTERS):
        taps = taps_for(SPREADS[s], k)
        for y in range(64):
            one[y : y + 21, f, y] = taps
    two = one.reshape(SPAN, 6, 2, 64)[:, :, ::-1]
    both = np.stack([one.reshape(SPAN, LANES), two.reshape(SPAN, LANES)])
    high = both.astype(jnp.bfloat16)
    low = (both - high.astype(np.float32)).astype(jnp.bfloat16)
    out = np.zeros((2, 256, LANES), jnp.bfloat16)
    out[:, 0:SPAN], out[:, SPAN : 2 * SPAN], out[:, 2 * SPAN : 3 * SPAN] = high, high, low
    return out


def row_filters():
    out = np.zeros((MAXI, M, NF, CH), np.float32)
    for f, (s, k) in enumerate(FILTERS):
        for i in range(DEGREES[s] + 1 - k):
            taps = taps_for(SPREADS[s], i)
            for x in range(M):
                out[i, x, f, x + ROFF : x + ROFF + 21] = taps
    return out.reshape(MAXI, M, KK)


def split(value):
    high = value.astype(jnp.bfloat16)
    low = (value - high.astype(jnp.float32)).astype(jnp.bfloat16)
    return high, low


def mix_kernel(coef_ref, rows_ref, flat_ref, slope_ref):
    def mixed(g):
        total = coef_ref[0, g, 0:1, :] * rows_ref[0]
        for i in range(1, MAXI):
            total = total + coef_ref[0, g, i : i + 1, :] * rows_ref[i]
        return total

    const, across, down = mixed(0), mixed(1), mixed(2)
    high, low = split(across)
    slope_ref[0, 0:M, :] = high
    slope_ref[0, M : 2 * M, :] = low
    half = (BLK - 1) / 2.0
    for t in range(NT):
        row = lax.broadcasted_iota(jnp.int32, (M, 1), 0) + t * M
        weight = (row.astype(jnp.float32) - half) * (1.0 / half)
        high, low = split(const + weight * down)
        flat_ref[0, t, 0:M, :] = high
        flat_ref[0, t, M : 2 * M, :] = low


def coefficient_rows(coeffs):
    index = np.zeros((MAXI, NF), np.int32)
    valid = np.zeros((MAXI, NF), np.float32)
    for f, (s, k) in enumerate(FILTERS):
        for i in range(DEGREES[s] + 1 - k):
            index[i, f] = BASIS[(s, i, k)]
            valid[i, f] = 1.0
    picked = jnp.stack(
        [jnp.stack([coeffs[:, int(index[i, f]), :] * float(valid[i, f]) for f in range(NF)], 1) for i in range(MAXI)], 1
    )
    return jnp.repeat(jnp.transpose(picked, (0, 3, 1, 2)), CH, axis=3)


def mix_rows(lanes):
    nb = lanes.shape[0]
    return pl.pallas_call(
        mix_kernel,
        grid=(nb,),
        in_specs=[
            pl.BlockSpec((1, 3, MAXI, KK), lambda b: (b, 0, 0, 0)),
            pl.BlockSpec((MAXI, M, KK), lambda b: (0, 0, 0)),
        ],
        out_specs=[
            pl.BlockSpec((1, NT, 2 * M, KK), lambda b: (b, 0, 0, 0)),
            pl.BlockSpec((1, 2 * M, KK), lambda b: (b, 0, 0)),
        ],
        out_shape=[
            jax.ShapeDtypeStruct((nb, NT, 2 * M, KK), jnp.bfloat16),
            jax.ShapeDtypeStruct((nb, 2 * M, KK), jnp.bfloat16),
        ],
        name="mix_rows",
        cost_estimate=pl.CostEstimate(flops=10**8, bytes_accessed=2 * 10**7, transcendentals=0),
    )(lanes, jnp.asarray(row_filters()))


def model_kernel(index_ref, line_ref, *refs):
    pieces = refs[:PIECES]
    warped_ref, flat_ref, slope_ref, cols_ref, out_ref, image, packed, vh, vl, sem = refs[PIECES:]
    n = pl.program_id(0)

    @pl.when(n == 0)
    def _():
        copies = []
        for p, (start, size) in enumerate(PLACES):
            copies.append(pltpu.make_async_copy(pieces[p], image.at[pl.ds(start, size)], sem.at[p]))
        for copy in copies:
            copy.start()
        for copy in copies:
            copy.wait()

    q, h, my_y = line_ref[3 * n], line_ref[3 * n + 1], line_ref[3 * n + 2]
    strips = [(0, 3, 48, 16, q > 0)] + [(1, k, 0, 64, None) for k in range(4)] + [(2, 0, 0, 16, q < 7)]
    lane = lax.broadcasted_iota(jnp.int32, (64, 128), 1)
    at = 0
    for a, k, first, height, inside in strips:
        d = lax.rem(k - my_y + 4, 4)
        rows = pl.ds(first, height)
        left = image[index_ref[n * 9 + 3 * a], d, rows, 128:256]
        body = image[index_ref[n * 9 + 3 * a + 1], d, rows, :]
        right = image[index_ref[n * 9 + 3 * a + 2], d, rows, 0:128]
        left = jnp.where(h > 0, left, 0.0)
        right = jnp.where(h < 7, right, 0.0)
        wide = jnp.concatenate([left, body, right], axis=1)
        if inside is not None:
            wide = jnp.where(inside, wide, 0.0)
        where = lane[0:height]
        for t in range(4):
            moved = pltpu.roll(wide, WC - COFF - 64 * (t % 2), axis=1)
            value = moved[:, 128 * (t // 2) : 128 * (t // 2) + 128]
            high = value.astype(jnp.bfloat16).astype(jnp.float32)
            low = pltpu.roll(value - high, SPAN, axis=1)
            again = pltpu.roll(high, 2 * SPAN - 128, axis=1)
            packed[t, at : at + height, 0:128] = jnp.where(where < SPAN, high, low).astype(jnp.bfloat16)
            packed[t, at : at + height, 128:256] = jnp.where(where < 2 * SPAN - 128, low, again).astype(jnp.bfloat16)
        at += height

    lane = lax.broadcasted_iota(jnp.int32, (WR, 128), 1)
    for half in range(2):
        for g in range(3):
            lanes = slice(256 * g, 256 * g + 256)
            one = jnp.dot(packed[2 * half], cols_ref[0, :, lanes], preferred_element_type=jnp.float32)
            two = jnp.dot(packed[2 * half + 1], cols_ref[1, :, lanes], preferred_element_type=jnp.float32)
            for p in range(2):
                f = 4 * g + 2 * p
                first, second = one[:, 128 * p : 128 * p + 128], two[:, 128 * p : 128 * p + 128]
                high, low = split(jnp.where(lane < 64, first, second))
                vh[f, :, 128 * half : 128 * (half + 1)] = high
                vl[f, :, 128 * half : 128 * (half + 1)] = low
                if f + 1 < NF:
                    high, low = split(pltpu.roll(jnp.where(lane < 64, second, first), 64, axis=1))
                    vh[f + 1, :, 128 * half : 128 * (half + 1)] = high
                    vl[f + 1, :, 128 * half : 128 * (half + 1)] = low

    mid = (BLK - 1) / 2.0
    across = (lax.broadcasted_iota(jnp.int32, (1, BLK), 1).astype(jnp.float32) - mid) * (1.0 / mid)
    for t in range(NT):
        start = t * M
        wh = vh[:, start : start + CH, :].reshape(KK, BLK)
        wl = vl[:, start : start + CH, :].reshape(KK, BLK)
        lhs = jnp.concatenate([flat_ref[0, t, 0:M], slope_ref[0, 0:M], flat_ref[0, t, M : 2 * M], slope_ref[0, M : 2 * M]], axis=0)
        first = jnp.dot(lhs, wh, preferred_element_type=jnp.float32)
        second = jnp.dot(lhs[0 : 2 * M], wl, preferred_element_type=jnp.float32)
        flat = first[0:M] + first[2 * M : 3 * M] + second[0:M]
        slope = first[M : 2 * M] + first[3 * M : 4 * M] + second[M : 2 * M]
        out_ref[0, start : start + M, :] = warped_ref[0, start : start + M, :] - (flat + across * slope)


def difference(pieces, warped, rows, index, line):
    nb = warped.shape[0]
    spec = pltpu.PrefetchScalarGridSpec(
        num_scalar_prefetch=2,
        grid=(nb,),
        in_specs=[pl.BlockSpec(memory_space=pl.ANY)] * PIECES
        + [
            pl.BlockSpec((1, BLK, BLK), lambda b, *_: (b, 0, 0)),
            pl.BlockSpec((1, NT, 2 * M, KK), lambda b, *_: (b, 0, 0, 0)),
            pl.BlockSpec((1, 2 * M, KK), lambda b, *_: (b, 0, 0)),
            pl.BlockSpec((2, 256, LANES), lambda b, *_: (0, 0, 0)),
        ],
        out_specs=pl.BlockSpec((1, BLK, BLK), lambda b, *_: (b, 0, 0)),
        scratch_shapes=[
            pltpu.VMEM((64, 4, 64, BLK), jnp.float32),
            pltpu.VMEM((4, WR, 256), jnp.bfloat16),
            pltpu.VMEM((NF, WR, BLK), jnp.bfloat16),
            pltpu.VMEM((NF, WR, BLK), jnp.bfloat16),
            pltpu.SemaphoreType.DMA((PIECES,)),
        ],
    )
    return pl.pallas_call(
        model_kernel,
        grid_spec=spec,
        out_shape=jax.ShapeDtypeStruct((nb, BLK, BLK), jnp.float32),
        name="difference",
    )(index, line, *pieces, warped, *rows, jnp.asarray(column_filters()))


AXES = ("trow", "tcol", "visit")


def device_of(x, y, z, core):
    return ((x % 2 * 2 + core) * 4 + z) * 8 + x // 2 * 4 + y


def fetch(value, x=0, y=0, z=0, core=0):
    pairs = []
    for i in range(4):
        for j in range(4):
            for k in range(4):
                for c in range(2):
                    source = device_of((i + x) % 4, (j + y) % 4, (k + z) % 4, (c + core) % 2)
                    pairs.append((source, device_of(i, j, k, c)))
    return lax.ppermute(value, AXES, pairs)


def ring(value, axis):
    return [value] + [fetch(value, **{axis: d}) for d in (1, 2, 3)]


PLACES = [(((half * 4 + ds) * 2 + dc) * 4 + d1, 2) for half in range(2) for ds in range(4) for dc in range(2) for d1 in (0, 2)]
PIECES = len(PLACES)


def gather_template(template, small, mix):
    strips, small = lax.optimization_barrier((jnp.stack(ring(template, "y")), small))
    rows = mix(small)
    parts = []
    for half, (first, second) in enumerate((("x", "z"), ("z", "x"))):
        square = ring(strips[:, :, half * BLK : (half + 1) * BLK], first)
        a, b = jnp.stack(square[:2]), jnp.stack(square[2:])
        near_a, last_b = fetch(a, **{second: 1}), fetch(b, **{second: 3})
        near_b, last_a = fetch(b, **{second: 1}), fetch(a, **{second: 3})
        if half == 0:
            near_a, rows = lax.optimization_barrier((near_a, rows))
        far_a, far_b = fetch(near_a, **{second: 1}), fetch(last_b, **{second: 3})
        for pair in ((a, b), (near_a, near_b), (far_a, far_b), (last_a, last_b)):
            parts.extend(pair)
            parts.extend(fetch(p, core=1) for p in pair)
    return parts, small, rows


def sub_index(q, h):
    trow, visit = lax.axis_index("trow"), lax.axis_index("visit")
    my_x, my_z, my_core = visit // 4 * 2 + trow // 2, lax.axis_index("tcol"), trow % 2
    tile_row, tile_col = q // 2, h // 2
    dx = (q % 2 * 2 + tile_row // 2 - my_x + 4) % 4
    dz = (tile_col - my_z + 4) % 4
    dc = (tile_row % 2 - my_core + 2) % 2
    by_z = (dz * 2 + dc) * 4 + dx
    by_x = 32 + (dx * 2 + dc) * 4 + dz
    return jnp.where(h % 2 == 0, by_z, by_x)


def window_index(dest_tile, position):
    q = dest_tile // 4 * 2 + position // 2
    h = dest_tile % 4 * 2 + position % 2
    near = jnp.array([-1, 0, 1], jnp.int32)
    rows = jnp.clip(q[:, None, None] + near[None, :, None], 0, 7)
    cols = jnp.clip(h[:, None, None] + near[None, None, :], 0, 7)
    index = sub_index(rows, cols).reshape(-1).astype(jnp.int32)
    my_y = jnp.broadcast_to(lax.axis_index("visit") % 4, q.shape)
    return index, jnp.stack([q, h, my_y], axis=1).reshape(-1).astype(jnp.int32)


def on_device(template, warped, coeffs, dest_tile, position):
    index, line = window_index(dest_tile[:, 0], position[:, 0])
    small = (index, line, coefficient_rows(coeffs))
    pieces, (index, line, _), rows = gather_template(template, small, lambda small: mix_rows(small[2]))
    return difference(pieces, warped, rows, index, line)


def solution(mesh):
    return jax.shard_map(
        on_device,
        mesh=mesh,
        in_specs=(
            P(("trow", "visit"), "tcol"),
            P(("trow", "tcol", "visit"), None, None),
            P(("trow", "tcol", "visit"), None, None),
            P(("trow", "tcol", "visit"), None),
            P(("trow", "tcol", "visit"), None),
        ),
        out_specs=P(("trow", "tcol", "visit"), None, None),
        check_vma=False,
    )
```

```python
import jax
import jax.numpy as jnp
import numpy as np
from jax import lax
from jax.experimental import pallas as pl
from jax.experimental.pallas import tpu as pltpu
from jax.sharding import PartitionSpec as P

BLK = 256
HALF = 10
SPREADS = (1.0, 2.0, 4.0)
DEGREES = (4, 2, 2)
FILTERS = [(s, k) for s, d in enumerate(DEGREES) for k in range(d + 1)]
NF = len(FILTERS)
BASIS = {}
for _s, _d in enumerate(DEGREES):
    for _i in range(_d + 1):
        for _j in range(_d + 1 - _i):
            BASIS[(_s, _i, _j)] = len(BASIS)
MAXI = max(DEGREES) + 1

M = 32
CH = M + 32
SPAN = 84
LANES = 768
NT = BLK // M
KK = NF * CH
WR = 288
WC = 512
ROFF = 16 - HALF
COFF = 128 - HALF


def taps_for(spread, power):
    offsets = np.arange(-HALF, HALF + 1).astype(np.float32)
    weights = np.exp(-offsets * offsets / np.float32(2.0 * spread * spread)).astype(np.float32)
    for _ in range(power):
        weights = weights * offsets
    return (weights / np.sqrt(np.sum(weights * weights))).astype(np.float32)


def column_filters():
    one = np.zeros((SPAN, 12, 64), np.float32)
    for f, (s, k) in enumerate(FILTERS):
        taps = taps_for(SPREADS[s], k)
        for y in range(64):
            one[y : y + 21, f, y] = taps
    two = one.reshape(SPAN, 6, 2, 64)[:, :, ::-1]
    both = np.stack([one.reshape(SPAN, LANES), two.reshape(SPAN, LANES)])
    high = both.astype(jnp.bfloat16)
    low = (both - high.astype(np.float32)).astype(jnp.bfloat16)
    out = np.zeros((2, 256, LANES), jnp.bfloat16)
    out[:, 0:SPAN], out[:, SPAN : 2 * SPAN], out[:, 2 * SPAN : 3 * SPAN] = high, high, low
    return out


def row_filters():
    out = np.zeros((MAXI, M, NF, CH), np.float32)
    for f, (s, k) in enumerate(FILTERS):
        for i in range(DEGREES[s] + 1 - k):
            taps = taps_for(SPREADS[s], i)
            for x in range(M):
                out[i, x, f, x + ROFF : x + ROFF + 21] = taps
    return out.reshape(MAXI, M, KK)


def split(value):
    high = value.astype(jnp.bfloat16)
    low = (value - high.astype(jnp.float32)).astype(jnp.bfloat16)
    return high, low


def mix_kernel(coef_ref, rows_ref, flat_ref, slope_ref):
    def mixed(g):
        total = coef_ref[0, g, 0:1, :] * rows_ref[0]
        for i in range(1, MAXI):
            total = total + coef_ref[0, g, i : i + 1, :] * rows_ref[i]
        return total

    const, across, down = mixed(0), mixed(1), mixed(2)
    high, low = split(across)
    slope_ref[0, 0:M, :] = high
    slope_ref[0, M : 2 * M, :] = low
    half = (BLK - 1) / 2.0
    for t in range(NT):
        row = lax.broadcasted_iota(jnp.int32, (M, 1), 0) + t * M
        weight = (row.astype(jnp.float32) - half) * (1.0 / half)
        high, low = split(const + weight * down)
        flat_ref[0, t, 0:M, :] = high
        flat_ref[0, t, M : 2 * M, :] = low


def coefficient_rows(coeffs):
    index = np.zeros((MAXI, NF), np.int32)
    valid = np.zeros((MAXI, NF), np.float32)
    for f, (s, k) in enumerate(FILTERS):
        for i in range(DEGREES[s] + 1 - k):
            index[i, f] = BASIS[(s, i, k)]
            valid[i, f] = 1.0
    picked = jnp.stack(
        [jnp.stack([coeffs[:, int(index[i, f]), :] * float(valid[i, f]) for f in range(NF)], 1) for i in range(MAXI)], 1
    )
    return jnp.repeat(jnp.transpose(picked, (0, 3, 1, 2)), CH, axis=3)


def mix_rows(lanes):
    nb = lanes.shape[0]
    return pl.pallas_call(
        mix_kernel,
        grid=(nb,),
        in_specs=[
            pl.BlockSpec((1, 3, MAXI, KK), lambda b: (b, 0, 0, 0)),
            pl.BlockSpec((MAXI, M, KK), lambda b: (0, 0, 0)),
        ],
        out_specs=[
            pl.BlockSpec((1, NT, 2 * M, KK), lambda b: (b, 0, 0, 0)),
            pl.BlockSpec((1, 2 * M, KK), lambda b: (b, 0, 0)),
        ],
        out_shape=[
            jax.ShapeDtypeStruct((nb, NT, 2 * M, KK), jnp.bfloat16),
            jax.ShapeDtypeStruct((nb, 2 * M, KK), jnp.bfloat16),
        ],
        name="mix_rows",
        cost_estimate=pl.CostEstimate(flops=10**8, bytes_accessed=2 * 10**7, transcendentals=0),
    )(lanes, jnp.asarray(row_filters()))


def model_kernel(index_ref, line_ref, *refs):
    pieces = refs[:PIECES]
    warped_ref, flat_ref, slope_ref, cols_ref, out_ref, image, packed, vh, vl, sem = refs[PIECES:]
    n = pl.program_id(0)

    @pl.when(n == 0)
    def _():
        copies = []
        for p, (start, size) in enumerate(PLACES):
            copies.append(pltpu.make_async_copy(pieces[p], image.at[pl.ds(start, size)], sem.at[p]))
        for copy in copies:
            copy.start()
        for copy in copies:
            copy.wait()

    q, h, my_y = line_ref[3 * n], line_ref[3 * n + 1], line_ref[3 * n + 2]
    strips = [(0, 3, 48, 16, q > 0)] + [(1, k, 0, 64, None) for k in range(4)] + [(2, 0, 0, 16, q < 7)]
    lane = lax.broadcasted_iota(jnp.int32, (64, 128), 1)
    at = 0
    for a, k, first, height, inside in strips:
        d = lax.rem(k - my_y + 4, 4)
        rows = pl.ds(first, height)
        left = image[index_ref[n * 9 + 3 * a], d, rows, 128:256]
        body = image[index_ref[n * 9 + 3 * a + 1], d, rows, :]
        right = image[index_ref[n * 9 + 3 * a + 2], d, rows, 0:128]
        left = jnp.where(h > 0, left, 0.0)
        right = jnp.where(h < 7, right, 0.0)
        wide = jnp.concatenate([left, body, right], axis=1)
        if inside is not None:
            wide = jnp.where(inside, wide, 0.0)
        where = lane[0:height]
        for t in range(4):
            moved = pltpu.roll(wide, WC - COFF - 64 * (t % 2), axis=1)
            value = moved[:, 128 * (t // 2) : 128 * (t // 2) + 128]
            high = value.astype(jnp.bfloat16).astype(jnp.float32)
            low = pltpu.roll(value - high, SPAN, axis=1)
            again = pltpu.roll(high, 2 * SPAN - 128, axis=1)
            packed[t, at : at + height, :] = jnp.concatenate(
                [jnp.where(where < SPAN, high, low), jnp.where(where < 2 * SPAN - 128, low, again)], axis=1
            ).astype(jnp.bfloat16)
        at += height

    lane = lax.broadcasted_iota(jnp.int32, (WR, 128), 1)
    for g in range(3):
        lanes = slice(256 * g, 256 * g + 256)
        passed = [jnp.dot(packed[t], cols_ref[t % 2, :, lanes], preferred_element_type=jnp.float32) for t in range(4)]
        for p in range(2):
            f = 4 * g + 2 * p
            cut = [value[:, 128 * p : 128 * p + 128] for value in passed]
            straight = [jnp.where(lane < 64, cut[0], cut[1]), jnp.where(lane < 64, cut[2], cut[3])]
            vh[f], vl[f] = split(jnp.concatenate(straight, axis=1))
            if f + 1 < NF:
                swapped = [jnp.where(lane < 64, cut[1], cut[0]), jnp.where(lane < 64, cut[3], cut[2])]
                vh[f + 1], vl[f + 1] = split(jnp.concatenate([pltpu.roll(v, 64, axis=1) for v in swapped], axis=1))

    mid = (BLK - 1) / 2.0
    across = (lax.broadcasted_iota(jnp.int32, (1, BLK), 1).astype(jnp.float32) - mid) * (1.0 / mid)
    for t in range(NT):
        start = t * M
        wh = vh[:, start : start + CH, :].reshape(KK, BLK)
        wl = vl[:, start : start + CH, :].reshape(KK, BLK)
        lhs = jnp.concatenate([flat_ref[0, t, 0:M], slope_ref[0, 0:M], flat_ref[0, t, M : 2 * M], slope_ref[0, M : 2 * M]], axis=0)
        first = jnp.dot(lhs, wh, preferred_element_type=jnp.float32)
        second = jnp.dot(lhs[0 : 2 * M], wl, preferred_element_type=jnp.float32)
        flat = first[0:M] + first[2 * M : 3 * M] + second[0:M]
        slope = first[M : 2 * M] + first[3 * M : 4 * M] + second[M : 2 * M]
        out_ref[0, start : start + M, :] = warped_ref[0, start : start + M, :] - (flat + across * slope)


def difference(pieces, warped, rows, index, line):
    nb = warped.shape[0]
    spec = pltpu.PrefetchScalarGridSpec(
        num_scalar_prefetch=2,
        grid=(nb,),
        in_specs=[pl.BlockSpec(memory_space=pl.ANY)] * PIECES
        + [
            pl.BlockSpec((1, BLK, BLK), lambda b, *_: (b, 0, 0)),
            pl.BlockSpec((1, NT, 2 * M, KK), lambda b, *_: (b, 0, 0, 0)),
            pl.BlockSpec((1, 2 * M, KK), lambda b, *_: (b, 0, 0)),
            pl.BlockSpec((2, 256, LANES), lambda b, *_: (0, 0, 0)),
        ],
        out_specs=pl.BlockSpec((1, BLK, BLK), lambda b, *_: (b, 0, 0)),
        scratch_shapes=[
            pltpu.VMEM((64, 4, 64, BLK), jnp.float32),
            pltpu.VMEM((4, WR, 256), jnp.bfloat16),
            pltpu.VMEM((NF, WR, BLK), jnp.bfloat16),
            pltpu.VMEM((NF, WR, BLK), jnp.bfloat16),
            pltpu.SemaphoreType.DMA((PIECES,)),
        ],
    )
    return pl.pallas_call(
        model_kernel,
        grid_spec=spec,
        out_shape=jax.ShapeDtypeStruct((nb, BLK, BLK), jnp.float32),
        name="difference",
        compiler_params=pltpu.CompilerParams(vmem_limit_bytes=36 * 2**20),
    )(index, line, *pieces, warped, *rows, jnp.asarray(column_filters()))


AXES = ("trow", "tcol", "visit")


def device_of(x, y, z, core):
    return ((x % 2 * 2 + core) * 4 + z) * 8 + x // 2 * 4 + y


def fetch(value, x=0, y=0, z=0, core=0):
    pairs = []
    for i in range(4):
        for j in range(4):
            for k in range(4):
                for c in range(2):
                    source = device_of((i + x) % 4, (j + y) % 4, (k + z) % 4, (c + core) % 2)
                    pairs.append((source, device_of(i, j, k, c)))
    return lax.ppermute(value, AXES, pairs)


def ring(value, axis):
    return [value] + [fetch(value, **{axis: d}) for d in (1, 2, 3)]


PLACES = [(((half * 4 + ds) * 2 + dc) * 4 + d1, 2) for half in range(2) for ds in range(4) for dc in range(2) for d1 in (0, 2)]
PIECES = len(PLACES)


def gather_template(template, lanes, lines):
    strips, lanes = lax.optimization_barrier((jnp.stack(ring(template, "y")), lanes))
    halves, parts = [], []
    for half, (first, second) in enumerate((("x", "z"), ("z", "x"))):
        square = ring(strips[:, :, half * BLK : (half + 1) * BLK], first)
        a, b = jnp.stack(square[:2]), jnp.stack(square[2:])
        near_a = fetch(a, **{second: 1})
        last_b = fetch(b, **{second: 3})
        near_b = fetch(b, **{second: 1})
        last_a = fetch(a, **{second: 3})
        halves.append([a, b, near_a, near_b, last_a, last_b])
    rows = mix_rows(lanes)
    halves[0][2], rows, lines = lax.optimization_barrier((halves[0][2], rows, lines))
    for half, second in enumerate(("z", "x")):
        a, b, near_a, near_b, last_a, last_b = halves[half]
        far_a = fetch(near_a, **{second: 1})
        far_b = fetch(last_b, **{second: 3})
        for pair in ((a, b), (near_a, near_b), (far_a, far_b), (last_a, last_b)):
            parts.extend(pair)
            for p in pair:
                parts.append(fetch(p, core=1))
    return parts, lines, rows


def sub_index(q, h):
    trow, visit = lax.axis_index("trow"), lax.axis_index("visit")
    my_x, my_z, my_core = visit // 4 * 2 + trow // 2, lax.axis_index("tcol"), trow % 2
    tile_row, tile_col = q // 2, h // 2
    dx = (q % 2 * 2 + tile_row // 2 - my_x + 4) % 4
    dz = (tile_col - my_z + 4) % 4
    dc = (tile_row % 2 - my_core + 2) % 2
    by_z = (dz * 2 + dc) * 4 + dx
    by_x = 32 + (dx * 2 + dc) * 4 + dz
    return jnp.where(h % 2 == 0, by_z, by_x)


def window_index(dest_tile, position):
    q = dest_tile // 4 * 2 + position // 2
    h = dest_tile % 4 * 2 + position % 2
    near = jnp.array([-1, 0, 1], jnp.int32)
    rows = jnp.clip(q[:, None, None] + near[None, :, None], 0, 7)
    cols = jnp.clip(h[:, None, None] + near[None, None, :], 0, 7)
    index = sub_index(rows, cols).reshape(-1).astype(jnp.int32)
    my_y = jnp.broadcast_to(lax.axis_index("visit") % 4, q.shape)
    return index, jnp.stack([q, h, my_y], axis=1).reshape(-1).astype(jnp.int32)


def on_device(template, warped, coeffs, dest_tile, position):
    lines = window_index(dest_tile[:, 0], position[:, 0])
    pieces, (index, line), rows = gather_template(template, coefficient_rows(coeffs), lines)
    return difference(pieces, warped, rows, index, line)


def solution(mesh):
    return jax.shard_map(
        on_device,
        mesh=mesh,
        in_specs=(
            P(("trow", "visit"), "tcol"),
            P(("trow", "tcol", "visit"), None, None),
            P(("trow", "tcol", "visit"), None, None),
            P(("trow", "tcol", "visit"), None),
            P(("trow", "tcol", "visit"), None),
        ),
        out_specs=P(("trow", "tcol", "visit"), None, None),
        check_vma=False,
    )
```

```python
import jax
import jax.numpy as jnp
import numpy as np
from jax import lax
from jax.experimental import pallas as pl
from jax.experimental.pallas import tpu as pltpu
from jax.sharding import PartitionSpec as P

BLK = 256
HALF = 10
SPREADS = (1.0, 2.0, 4.0)
DEGREES = (4, 2, 2)
FILTERS = [(s, k) for s, d in enumerate(DEGREES) for k in range(d + 1)]
NF = len(FILTERS)
BASIS = {}
for _s, _d in enumerate(DEGREES):
    for _i in range(_d + 1):
        for _j in range(_d + 1 - _i):
            BASIS[(_s, _i, _j)] = len(BASIS)
MAXI = max(DEGREES) + 1

M = 32
CH = M + 32
SPAN = 84
LANES = 768
NT = BLK // M
KK = NF * CH
WR = 288
WC = 512
ROFF = 16 - HALF
COFF = 128 - HALF


def taps_for(spread, power):
    offsets = np.arange(-HALF, HALF + 1).astype(np.float32)
    weights = np.exp(-offsets * offsets / np.float32(2.0 * spread * spread)).astype(np.float32)
    for _ in range(power):
        weights = weights * offsets
    return (weights / np.sqrt(np.sum(weights * weights))).astype(np.float32)


def column_filters():
    one = np.zeros((SPAN, 12, 64), np.float32)
    for f, (s, k) in enumerate(FILTERS):
        taps = taps_for(SPREADS[s], k)
        for y in range(64):
            one[y : y + 21, f, y] = taps
    two = one.reshape(SPAN, 6, 2, 64)[:, :, ::-1]
    both = np.stack([one.reshape(SPAN, LANES), two.reshape(SPAN, LANES)])
    high = both.astype(jnp.bfloat16)
    low = (both - high.astype(np.float32)).astype(jnp.bfloat16)
    out = np.zeros((2, 256, LANES), jnp.bfloat16)
    out[:, 0:SPAN], out[:, SPAN : 2 * SPAN], out[:, 2 * SPAN : 3 * SPAN] = high, high, low
    return out


def row_filters():
    out = np.zeros((MAXI, M, NF, CH), np.float32)
    for f, (s, k) in enumerate(FILTERS):
        for i in range(DEGREES[s] + 1 - k):
            taps = taps_for(SPREADS[s], i)
            for x in range(M):
                out[i, x, f, x + ROFF : x + ROFF + 21] = taps
    return out.reshape(MAXI, M, KK)


def split(value):
    high = value.astype(jnp.bfloat16)
    low = (value - high.astype(jnp.float32)).astype(jnp.bfloat16)
    return high, low


MIX = 2


def mix_kernel(coef_ref, rows_ref, out_ref):
    half = (BLK - 1) / 2.0
    for k in range(MIX):

        def mixed(g):
            total = coef_ref[k, 5 * g : 5 * g + 1, :] * rows_ref[0]
            for i in range(1, MAXI):
                total = total + coef_ref[k, 5 * g + i : 5 * g + i + 1, :] * rows_ref[i]
            return total

        const, across, down = mixed(0), mixed(1), mixed(2)
        high, low = split(across)
        out_ref[k, NT, 0:M, :] = high
        out_ref[k, NT, M : 2 * M, :] = low
        for t in range(NT):
            row = lax.broadcasted_iota(jnp.int32, (M, 1), 0) + t * M
            weight = (row.astype(jnp.float32) - half) * (1.0 / half)
            high, low = split(const + weight * down)
            out_ref[k, t, 0:M, :] = high
            out_ref[k, t, M : 2 * M, :] = low


def coefficient_rows(coeffs):
    index = np.zeros((MAXI, NF), np.int32)
    valid = np.zeros((MAXI, NF), np.float32)
    for f, (s, k) in enumerate(FILTERS):
        for i in range(DEGREES[s] + 1 - k):
            index[i, f] = BASIS[(s, i, k)]
            valid[i, f] = 1.0
    picked = jnp.stack(
        [jnp.stack([coeffs[:, int(index[i, f]), :] * float(valid[i, f]) for f in range(NF)], 1) for i in range(MAXI)], 1
    )
    table = jnp.transpose(picked, (0, 3, 1, 2)).reshape(-1, 3 * MAXI, NF)
    table = jnp.pad(table, ((0, 0), (0, 1), (0, 0)))
    return jnp.repeat(table, CH, axis=2)


def mix_rows(lanes):
    nb = lanes.shape[0]
    return pl.pallas_call(
        mix_kernel,
        grid=(nb // MIX,),
        in_specs=[
            pl.BlockSpec((MIX, 16, KK), lambda b: (b, 0, 0)),
            pl.BlockSpec((MAXI, M, KK), lambda b: (0, 0, 0)),
        ],
        out_specs=pl.BlockSpec((MIX, NT + 1, 2 * M, KK), lambda b: (b, 0, 0, 0)),
        out_shape=jax.ShapeDtypeStruct((nb, NT + 1, 2 * M, KK), jnp.bfloat16),
        name="mix_rows",
        cost_estimate=pl.CostEstimate(flops=10**8, bytes_accessed=2 * 10**7, transcendentals=0),
    )(lanes, jnp.asarray(row_filters()))


def model_kernel(index_ref, line_ref, *refs):
    pieces = refs[:PIECES]
    warped_ref, mix_ref, cols_ref, out_ref, image, packed, vh, vl, sem = refs[PIECES:]
    n = pl.program_id(0)

    @pl.when(n == 0)
    def _():
        copies = []
        for p, (start, size) in enumerate(PLACES):
            copies.append(pltpu.make_async_copy(pieces[p], image.at[pl.ds(start, size)], sem.at[p]))
        for copy in copies:
            copy.start()
        for copy in copies:
            copy.wait()

    q, h, my_y = line_ref[3 * n], line_ref[3 * n + 1], line_ref[3 * n + 2]
    strips = [(0, 3, 48, 16, q > 0)] + [(1, k, 0, 64, None) for k in range(4)] + [(2, 0, 0, 16, q < 7)]
    lane = lax.broadcasted_iota(jnp.int32, (64, 128), 1)
    at = 0
    for a, k, first, height, inside in strips:
        d = lax.rem(k - my_y + 4, 4)
        rows = pl.ds(first, height)
        left = image[index_ref[n * 9 + 3 * a], d, rows, 128:256]
        body = image[index_ref[n * 9 + 3 * a + 1], d, rows, :]
        right = image[index_ref[n * 9 + 3 * a + 2], d, rows, 0:128]
        left = jnp.where(h > 0, left, 0.0)
        right = jnp.where(h < 7, right, 0.0)
        wide = jnp.concatenate([left, body, right], axis=1)
        if inside is not None:
            wide = jnp.where(inside, wide, 0.0)
        where = lane[0:height]
        for t in range(4):
            moved = pltpu.roll(wide, WC - COFF - 64 * (t % 2), axis=1)
            value = moved[:, 128 * (t // 2) : 128 * (t // 2) + 128]
            high = value.astype(jnp.bfloat16).astype(jnp.float32)
            low = pltpu.roll(value - high, SPAN, axis=1)
            again = pltpu.roll(high, 2 * SPAN - 128, axis=1)
            packed[t, at : at + height, :] = jnp.concatenate(
                [jnp.where(where < SPAN, high, low), jnp.where(where < 2 * SPAN - 128, low, again)], axis=1
            ).astype(jnp.bfloat16)
        at += height

    lane = lax.broadcasted_iota(jnp.int32, (WR, 128), 1)
    for g in range(3):
        lanes = slice(256 * g, 256 * g + 256)
        passed = [jnp.dot(packed[t], cols_ref[t % 2, :, lanes], preferred_element_type=jnp.float32) for t in range(4)]
        for p in range(2):
            f = 4 * g + 2 * p
            cut = [value[:, 128 * p : 128 * p + 128] for value in passed]
            straight = [jnp.where(lane < 64, cut[0], cut[1]), jnp.where(lane < 64, cut[2], cut[3])]
            vh[f], vl[f] = split(jnp.concatenate(straight, axis=1))
            if f + 1 < NF:
                swapped = [jnp.where(lane < 64, cut[1], cut[0]), jnp.where(lane < 64, cut[3], cut[2])]
                vh[f + 1], vl[f + 1] = split(jnp.concatenate([pltpu.roll(v, 64, axis=1) for v in swapped], axis=1))

    mid = (BLK - 1) / 2.0
    across = (lax.broadcasted_iota(jnp.int32, (1, BLK), 1).astype(jnp.float32) - mid) * (1.0 / mid)
    for t in range(NT):
        start = t * M
        wh = vh[:, start : start + CH, :].reshape(KK, BLK)
        wl = vl[:, start : start + CH, :].reshape(KK, BLK)
        lhs = jnp.concatenate([mix_ref[0, t, 0:M], mix_ref[0, NT, 0:M], mix_ref[0, t, M : 2 * M], mix_ref[0, NT, M : 2 * M]], axis=0)
        first = jnp.dot(lhs, wh, preferred_element_type=jnp.float32)
        second = jnp.dot(lhs[0 : 2 * M], wl, preferred_element_type=jnp.float32)
        flat = first[0:M] + first[2 * M : 3 * M] + second[0:M]
        slope = first[M : 2 * M] + first[3 * M : 4 * M] + second[M : 2 * M]
        out_ref[0, start : start + M, :] = warped_ref[0, start : start + M, :] - (flat + across * slope)


def difference(pieces, warped, rows, index, line):
    nb = warped.shape[0]
    spec = pltpu.PrefetchScalarGridSpec(
        num_scalar_prefetch=2,
        grid=(nb,),
        in_specs=[pl.BlockSpec(memory_space=pl.ANY)] * PIECES
        + [
            pl.BlockSpec((1, BLK, BLK), lambda b, *_: (b, 0, 0)),
            pl.BlockSpec((1, NT + 1, 2 * M, KK), lambda b, *_: (b, 0, 0, 0)),
            pl.BlockSpec((2, 256, LANES), lambda b, *_: (0, 0, 0)),
        ],
        out_specs=pl.BlockSpec((1, BLK, BLK), lambda b, *_: (b, 0, 0)),
        scratch_shapes=[
            pltpu.VMEM((64, 4, 64, BLK), jnp.float32),
            pltpu.VMEM((4, WR, 256), jnp.bfloat16),
            pltpu.VMEM((NF, WR, BLK), jnp.bfloat16),
            pltpu.VMEM((NF, WR, BLK), jnp.bfloat16),
            pltpu.SemaphoreType.DMA((PIECES,)),
        ],
    )
    return pl.pallas_call(
        model_kernel,
        grid_spec=spec,
        out_shape=jax.ShapeDtypeStruct((nb, BLK, BLK), jnp.float32),
        name="difference",
        compiler_params=pltpu.CompilerParams(vmem_limit_bytes=36 * 2**20),
    )(index, line, *pieces, warped, rows, jnp.asarray(column_filters()))


AXES = ("trow", "tcol", "visit")


def device_of(x, y, z, core):
    return ((x % 2 * 2 + core) * 4 + z) * 8 + x // 2 * 4 + y


def fetch(value, x=0, y=0, z=0, core=0):
    pairs = []
    for i in range(4):
        for j in range(4):
            for k in range(4):
                for c in range(2):
                    source = device_of((i + x) % 4, (j + y) % 4, (k + z) % 4, (c + core) % 2)
                    pairs.append((source, device_of(i, j, k, c)))
    return lax.ppermute(value, AXES, pairs)


def ring(value, axis):
    return [value] + [fetch(value, **{axis: d}) for d in (1, 2, 3)]


PLACES = [(((half * 4 + ds) * 2 + dc) * 4 + d1, 2) for half in range(2) for ds in range(4) for dc in range(2) for d1 in (0, 2)]
PIECES = len(PLACES)


def gather_template(template, lanes, lines):
    strips, lanes = lax.optimization_barrier((jnp.stack(ring(template, "y")), lanes))
    halves, parts = [], []
    for half, (first, second) in enumerate((("x", "z"), ("z", "x"))):
        square = ring(strips[:, :, half * BLK : (half + 1) * BLK], first)
        a, b = jnp.stack(square[:2]), jnp.stack(square[2:])
        near_a = fetch(a, **{second: 1})
        last_b = fetch(b, **{second: 3})
        near_b = fetch(b, **{second: 1})
        last_a = fetch(a, **{second: 3})
        halves.append([a, b, near_a, near_b, last_a, last_b])
    rows = mix_rows(lanes)
    halves[0][2], rows, lines = lax.optimization_barrier((halves[0][2], rows, lines))
    for half, second in enumerate(("z", "x")):
        a, b, near_a, near_b, last_a, last_b = halves[half]
        far_a = fetch(near_a, **{second: 1})
        far_b = fetch(last_b, **{second: 3})
        for pair in ((a, b), (near_a, near_b), (far_a, far_b), (last_a, last_b)):
            parts.extend(pair)
            for p in pair:
                parts.append(fetch(p, core=1))
    return parts, lines, rows


def sub_index(q, h):
    trow, visit = lax.axis_index("trow"), lax.axis_index("visit")
    my_x, my_z, my_core = visit // 4 * 2 + trow // 2, lax.axis_index("tcol"), trow % 2
    tile_row, tile_col = q // 2, h // 2
    dx = (q % 2 * 2 + tile_row // 2 - my_x + 4) % 4
    dz = (tile_col - my_z + 4) % 4
    dc = (tile_row % 2 - my_core + 2) % 2
    by_z = (dz * 2 + dc) * 4 + dx
    by_x = 32 + (dx * 2 + dc) * 4 + dz
    return jnp.where(h % 2 == 0, by_z, by_x)


def window_index(dest_tile, position):
    q = dest_tile // 4 * 2 + position // 2
    h = dest_tile % 4 * 2 + position % 2
    near = jnp.array([-1, 0, 1], jnp.int32)
    rows = jnp.clip(q[:, None, None] + near[None, :, None], 0, 7)
    cols = jnp.clip(h[:, None, None] + near[None, None, :], 0, 7)
    index = sub_index(rows, cols).reshape(-1).astype(jnp.int32)
    my_y = jnp.broadcast_to(lax.axis_index("visit") % 4, q.shape)
    return index, jnp.stack([q, h, my_y], axis=1).reshape(-1).astype(jnp.int32)


def on_device(template, warped, coeffs, dest_tile, position):
    lines = window_index(dest_tile[:, 0], position[:, 0])
    pieces, (index, line), rows = gather_template(template, coefficient_rows(coeffs), lines)
    return difference(pieces, warped, rows, index, line)


def solution(mesh):
    return jax.shard_map(
        on_device,
        mesh=mesh,
        in_specs=(
            P(("trow", "visit"), "tcol"),
            P(("trow", "tcol", "visit"), None, None),
            P(("trow", "tcol", "visit"), None, None),
            P(("trow", "tcol", "visit"), None),
            P(("trow", "tcol", "visit"), None),
        ),
        out_specs=P(("trow", "tcol", "visit"), None, None),
        check_vma=False,
    )
```

```python
import jax
import jax.numpy as jnp
import numpy as np
from jax import lax
from jax.experimental import pallas as pl
from jax.experimental.pallas import tpu as pltpu
from jax.sharding import PartitionSpec as P

BLK = 256
HALF = 10
SPREADS = (1.0, 2.0, 4.0)
DEGREES = (4, 2, 2)
FILTERS = [(s, k) for s, d in enumerate(DEGREES) for k in range(d + 1)]
NF = len(FILTERS)
BASIS = {}
for _s, _d in enumerate(DEGREES):
    for _i in range(_d + 1):
        for _j in range(_d + 1 - _i):
            BASIS[(_s, _i, _j)] = len(BASIS)
MAXI = max(DEGREES) + 1

M = 32
CH = M + 32
SPAN = 84
LANES = 768
NT = BLK // M
KK = NF * CH
WR = 288
WC = 512
ROFF = 16 - HALF
COFF = 128 - HALF


def taps_for(spread, power):
    offsets = np.arange(-HALF, HALF + 1).astype(np.float32)
    weights = np.exp(-offsets * offsets / np.float32(2.0 * spread * spread)).astype(np.float32)
    for _ in range(power):
        weights = weights * offsets
    return (weights / np.sqrt(np.sum(weights * weights))).astype(np.float32)


def column_filters():
    one = np.zeros((SPAN, 12, 64), np.float32)
    for f, (s, k) in enumerate(FILTERS):
        taps = taps_for(SPREADS[s], k)
        for y in range(64):
            one[y : y + 21, f, y] = taps
    two = one.reshape(SPAN, 6, 2, 64)[:, :, ::-1]
    both = np.stack([one.reshape(SPAN, LANES), two.reshape(SPAN, LANES)])
    high = both.astype(jnp.bfloat16)
    low = (both - high.astype(np.float32)).astype(jnp.bfloat16)
    out = np.zeros((2, 256, LANES), jnp.bfloat16)
    out[:, 0:SPAN], out[:, SPAN : 2 * SPAN], out[:, 2 * SPAN : 3 * SPAN] = high, high, low
    return out


def row_filters():
    out = np.zeros((MAXI, M, NF, CH), np.float32)
    for f, (s, k) in enumerate(FILTERS):
        for i in range(DEGREES[s] + 1 - k):
            taps = taps_for(SPREADS[s], i)
            for x in range(M):
                out[i, x, f, x + ROFF : x + ROFF + 21] = taps
    return out.reshape(MAXI, M, KK)


def split(value):
    high = value.astype(jnp.bfloat16)
    low = (value - high.astype(jnp.float32)).astype(jnp.bfloat16)
    return high, low


MIX = 4


def mix_kernel(coef_ref, rows_ref, out_ref):
    half = (BLK - 1) / 2.0
    for k in range(MIX):

        def mixed(g):
            total = coef_ref[k, 5 * g : 5 * g + 1, :] * rows_ref[0]
            for i in range(1, MAXI):
                total = total + coef_ref[k, 5 * g + i : 5 * g + i + 1, :] * rows_ref[i]
            return total

        const, across, down = mixed(0), mixed(1), mixed(2)
        high, low = split(across)
        out_ref[k, NT, 0:M, :] = high
        out_ref[k, NT, M : 2 * M, :] = low
        for t in range(NT):
            row = lax.broadcasted_iota(jnp.int32, (M, 1), 0) + t * M
            weight = (row.astype(jnp.float32) - half) * (1.0 / half)
            high, low = split(const + weight * down)
            out_ref[k, t, 0:M, :] = high
            out_ref[k, t, M : 2 * M, :] = low


def coefficient_rows(coeffs):
    index = np.zeros((MAXI, NF), np.int32)
    valid = np.zeros((MAXI, NF), np.float32)
    for f, (s, k) in enumerate(FILTERS):
        for i in range(DEGREES[s] + 1 - k):
            index[i, f] = BASIS[(s, i, k)]
            valid[i, f] = 1.0
    picked = jnp.stack(
        [jnp.stack([coeffs[:, int(index[i, f]), :] * float(valid[i, f]) for f in range(NF)], 1) for i in range(MAXI)], 1
    )
    table = jnp.transpose(picked, (0, 3, 1, 2)).reshape(-1, 3 * MAXI, NF)
    table = jnp.pad(table, ((0, 0), (0, 1), (0, 0)))
    return jnp.repeat(table, CH, axis=2)


def mix_rows(lanes):
    nb = lanes.shape[0]
    return pl.pallas_call(
        mix_kernel,
        grid=(nb // MIX,),
        in_specs=[
            pl.BlockSpec((MIX, 16, KK), lambda b: (b, 0, 0)),
            pl.BlockSpec((MAXI, M, KK), lambda b: (0, 0, 0)),
        ],
        out_specs=pl.BlockSpec((MIX, NT + 1, 2 * M, KK), lambda b: (b, 0, 0, 0)),
        out_shape=jax.ShapeDtypeStruct((nb, NT + 1, 2 * M, KK), jnp.bfloat16),
        name="mix_rows",
        cost_estimate=pl.CostEstimate(flops=10**8, bytes_accessed=2 * 10**7, transcendentals=0),
    )(lanes, jnp.asarray(row_filters()))


STEP = 3


def model_kernel(index_ref, line_ref, *refs):
    pieces = refs[:PIECES]
    warped_ref, mix_ref, cols_ref, out_ref, image, packed, vh, vl, sem = refs[PIECES:]
    n = pl.program_id(0)

    @pl.when(n == 0)
    def _():
        copies = []
        for p, (start, size) in enumerate(PLACES):
            copies.append(pltpu.make_async_copy(pieces[p], image.at[pl.ds(start, size)], sem.at[p]))
        for copy in copies:
            copy.start()
        for copy in copies:
            copy.wait()

    for k2 in range(STEP):
        m = n * STEP + k2
        q, h, my_y = line_ref[3 * m], line_ref[3 * m + 1], line_ref[3 * m + 2]
        strips = [(0, 3, 48, 16, q > 0)] + [(1, k, 0, 64, None) for k in range(4)] + [(2, 0, 0, 16, q < 7)]
        lane = lax.broadcasted_iota(jnp.int32, (64, 128), 1)
        at = 0
        for a, k, first, height, inside in strips:
            d = lax.rem(k - my_y + 4, 4)
            rows = pl.ds(first, height)
            left = image[index_ref[m * 9 + 3 * a], d, rows, 128:256]
            body = image[index_ref[m * 9 + 3 * a + 1], d, rows, :]
            right = image[index_ref[m * 9 + 3 * a + 2], d, rows, 0:128]
            left = jnp.where(h > 0, left, 0.0)
            right = jnp.where(h < 7, right, 0.0)
            wide = jnp.concatenate([left, body, right], axis=1)
            if inside is not None:
                wide = jnp.where(inside, wide, 0.0)
            where = lane[0:height]
            for t in range(4):
                moved = pltpu.roll(wide, WC - COFF - 64 * (t % 2), axis=1)
                value = moved[:, 128 * (t // 2) : 128 * (t // 2) + 128]
                high = value.astype(jnp.bfloat16).astype(jnp.float32)
                low = pltpu.roll(value - high, SPAN, axis=1)
                again = pltpu.roll(high, 2 * SPAN - 128, axis=1)
                packed[t, at : at + height, :] = jnp.concatenate(
                    [jnp.where(where < SPAN, high, low), jnp.where(where < 2 * SPAN - 128, low, again)], axis=1
                ).astype(jnp.bfloat16)
            at += height

        lane = lax.broadcasted_iota(jnp.int32, (WR, 128), 1)
        for g in range(3):
            lanes = slice(256 * g, 256 * g + 256)
            passed = [jnp.dot(packed[t], cols_ref[t % 2, :, lanes], preferred_element_type=jnp.float32) for t in range(4)]
            for p in range(2):
                f = 4 * g + 2 * p
                cut = [value[:, 128 * p : 128 * p + 128] for value in passed]
                straight = [jnp.where(lane < 64, cut[0], cut[1]), jnp.where(lane < 64, cut[2], cut[3])]
                vh[f], vl[f] = split(jnp.concatenate(straight, axis=1))
                if f + 1 < NF:
                    swapped = [jnp.where(lane < 64, cut[1], cut[0]), jnp.where(lane < 64, cut[3], cut[2])]
                    vh[f + 1], vl[f + 1] = split(jnp.concatenate([pltpu.roll(v, 64, axis=1) for v in swapped], axis=1))

        mid = (BLK - 1) / 2.0
        across = (lax.broadcasted_iota(jnp.int32, (1, BLK), 1).astype(jnp.float32) - mid) * (1.0 / mid)
        for t in range(NT):
            start = t * M
            wh = vh[:, start : start + CH, :].reshape(KK, BLK)
            wl = vl[:, start : start + CH, :].reshape(KK, BLK)
            lhs = jnp.concatenate([mix_ref[k2, t, 0:M], mix_ref[k2, NT, 0:M], mix_ref[k2, t, M : 2 * M], mix_ref[k2, NT, M : 2 * M]], axis=0)
            first = jnp.dot(lhs, wh, preferred_element_type=jnp.float32)
            second = jnp.dot(lhs[0 : 2 * M], wl, preferred_element_type=jnp.float32)
            flat = first[0:M] + first[2 * M : 3 * M] + second[0:M]
            slope = first[M : 2 * M] + first[3 * M : 4 * M] + second[M : 2 * M]
            out_ref[k2, start : start + M, :] = warped_ref[k2, start : start + M, :] - (flat + across * slope)


def difference(pieces, warped, rows, index, line):
    nb = warped.shape[0]
    spec = pltpu.PrefetchScalarGridSpec(
        num_scalar_prefetch=2,
        grid=(nb // STEP,),
        in_specs=[pl.BlockSpec(memory_space=pl.ANY)] * PIECES
        + [
            pl.BlockSpec((STEP, BLK, BLK), lambda b, *_: (b, 0, 0)),
            pl.BlockSpec((STEP, NT + 1, 2 * M, KK), lambda b, *_: (b, 0, 0, 0)),
            pl.BlockSpec((2, 256, LANES), lambda b, *_: (0, 0, 0)),
        ],
        out_specs=pl.BlockSpec((STEP, BLK, BLK), lambda b, *_: (b, 0, 0)),
        scratch_shapes=[
            pltpu.VMEM((64, 4, 64, BLK), jnp.float32),
            pltpu.VMEM((4, WR, 256), jnp.bfloat16),
            pltpu.VMEM((NF, WR, BLK), jnp.bfloat16),
            pltpu.VMEM((NF, WR, BLK), jnp.bfloat16),
            pltpu.SemaphoreType.DMA((PIECES,)),
        ],
    )
    return pl.pallas_call(
        model_kernel,
        grid_spec=spec,
        out_shape=jax.ShapeDtypeStruct((nb, BLK, BLK), jnp.float32),
        name="difference",
        compiler_params=pltpu.CompilerParams(vmem_limit_bytes=36 * 2**20),
    )(index, line, *pieces, warped, rows, jnp.asarray(column_filters()))


AXES = ("trow", "tcol", "visit")


def device_of(x, y, z, core):
    return ((x % 2 * 2 + core) * 4 + z) * 8 + x // 2 * 4 + y


def fetch(value, x=0, y=0, z=0, core=0):
    pairs = []
    for i in range(4):
        for j in range(4):
            for k in range(4):
                for c in range(2):
                    source = device_of((i + x) % 4, (j + y) % 4, (k + z) % 4, (c + core) % 2)
                    pairs.append((source, device_of(i, j, k, c)))
    return lax.ppermute(value, AXES, pairs)


def ring(value, axis):
    return [value] + [fetch(value, **{axis: d}) for d in (1, 2, 3)]


PLACES = [(((half * 4 + ds) * 2 + dc) * 4 + d1, 2) for half in range(2) for ds in range(4) for dc in range(2) for d1 in (0, 2)]
PIECES = len(PLACES)


def gather_template(template, lanes, lines):
    strips, lanes = lax.optimization_barrier((jnp.stack(ring(template, "y")), lanes))
    halves, parts = [], []
    for half, (first, second) in enumerate((("x", "z"), ("z", "x"))):
        square = ring(strips[:, :, half * BLK : (half + 1) * BLK], first)
        a, b = jnp.stack(square[:2]), jnp.stack(square[2:])
        near_a = fetch(a, **{second: 1})
        last_b = fetch(b, **{second: 3})
        near_b = fetch(b, **{second: 1})
        last_a = fetch(a, **{second: 3})
        halves.append([a, b, near_a, near_b, last_a, last_b])
    rows = mix_rows(lanes)
    halves[0][2], rows, lines = lax.optimization_barrier((halves[0][2], rows, lines))
    for half, second in enumerate(("z", "x")):
        a, b, near_a, near_b, last_a, last_b = halves[half]
        far_a = fetch(near_a, **{second: 1})
        far_b = fetch(last_b, **{second: 3})
        for pair in ((a, b), (near_a, near_b), (far_a, far_b), (last_a, last_b)):
            parts.extend(pair)
            for p in pair:
                parts.append(fetch(p, core=1))
    return parts, lines, rows


def sub_index(q, h):
    trow, visit = lax.axis_index("trow"), lax.axis_index("visit")
    my_x, my_z, my_core = visit // 4 * 2 + trow // 2, lax.axis_index("tcol"), trow % 2
    tile_row, tile_col = q // 2, h // 2
    dx = (q % 2 * 2 + tile_row // 2 - my_x + 4) % 4
    dz = (tile_col - my_z + 4) % 4
    dc = (tile_row % 2 - my_core + 2) % 2
    by_z = (dz * 2 + dc) * 4 + dx
    by_x = 32 + (dx * 2 + dc) * 4 + dz
    return jnp.where(h % 2 == 0, by_z, by_x)


def window_index(dest_tile, position):
    q = dest_tile // 4 * 2 + position // 2
    h = dest_tile % 4 * 2 + position % 2
    near = jnp.array([-1, 0, 1], jnp.int32)
    rows = jnp.clip(q[:, None, None] + near[None, :, None], 0, 7)
    cols = jnp.clip(h[:, None, None] + near[None, None, :], 0, 7)
    index = sub_index(rows, cols).reshape(-1).astype(jnp.int32)
    my_y = jnp.broadcast_to(lax.axis_index("visit") % 4, q.shape)
    return index, jnp.stack([q, h, my_y], axis=1).reshape(-1).astype(jnp.int32)


def on_device(template, warped, coeffs, dest_tile, position):
    lines = window_index(dest_tile[:, 0], position[:, 0])
    pieces, (index, line), rows = gather_template(template, coefficient_rows(coeffs), lines)
    return difference(pieces, warped, rows, index, line)


def solution(mesh):
    return jax.shard_map(
        on_device,
        mesh=mesh,
        in_specs=(
            P(("trow", "visit"), "tcol"),
            P(("trow", "tcol", "visit"), None, None),
            P(("trow", "tcol", "visit"), None, None),
            P(("trow", "tcol", "visit"), None),
            P(("trow", "tcol", "visit"), None),
        ),
        out_specs=P(("trow", "tcol", "visit"), None, None),
        check_vma=False,
    )
```
